32 devices in a mesh: grp: 4 (over x, core), dp: 4 (over z), seq: 2 (over y).
Axes of the slice: x: 2, y: 2, z: 4, core: 2. Of those that a mesh axis runs over, the one named last changes fastest.
Arguments:
- student_saved_input: bfloat16 [16, 256, 3584], P(('grp', 'dp'), 'seq'), may hold values from -6 to 6
- student_saved_query: bfloat16 [16, 256, 1792], P(('grp', 'dp'), 'seq'), may hold values from -600 to 600
- feature_cotangent: bfloat16 [16, 256, 1792], P(('grp', 'dp'), 'seq'), may hold values from -6 to 6
- feature_weights: bfloat16 [128, 896], replicated, may hold values from -0.5 to 0.5
- adapter_down_weight: bfloat16 [8, 3584], replicated, may hold values from -0.09375 to 0.09375
- adapter_up_weight: bfloat16 [8, 1792], replicated, may hold values from -0.09375 to 0.09375
- teacher_next_query: bfloat16 [16, 512, 1792], P(('grp', 'dp'), 'seq'), may hold values from -6 to 6
- teacher_next_key: bfloat16 [16, 512, 256], P(('grp', 'dp'), 'seq'), may hold values from -6 to 6
- teacher_next_value: bfloat16 [16, 512, 256], P(('grp', 'dp'), 'seq'), may hold values from -6 to 6
- positions: int32 [16, 512], P(('grp', 'dp'), 'seq'), may hold values from 0 to 511, each once within a row
Outputs:
- teacher_output: bfloat16 [16, 512, 1792], P(('grp', 'dp'), 'seq')
- grad_feature: float32 [128, 896], P('dp')
- grad_down: float32 [8, 3584], P(None, 'dp')
- up_gradient: float32 [8, 1792], P(None, 'dp')
The draws below stay inside these ranges and needn't reach their ends.
Inputs may be any that keep to these rules, and one draw needn't show every extreme that they name: `positions`: each sequence's row is a permutation of 0 to 511.
All inputs are finite; a program needn't handle non-finite values.
Results may differ from the reference program's by a relative error of at most 0.015.
Values may be sent and summed in bfloat16 or wider, within the bound.
No kernel may reach another device: no remote copies, remote signals or barrier semaphores. Data moves between devices by JAX's collectives and lax.ppermute only.
A program may use at most 64 MiB of HBM per device.

```python
import jax
import jax.numpy as jnp
from jax import lax

MODEL_WIDTH = 3584
QUERY_HEADS = 14
KEY_VALUE_HEADS = 2
HEAD_SIZE = 128
F = 64
LOW_RANK = 8
TEACHER_BATCH = 16
SBATCH = 16
TEACHER_LENGTH = 512
SLEN = 256


def teacher_pair(key):
    group_width = QUERY_HEADS // KEY_VALUE_HEADS
    rows_of_queries = jnp.clip(jax.random.normal(jax.random.fold_in(key, 101), (TEACHER_BATCH, TEACHER_LENGTH, KEY_VALUE_HEADS, group_width, HEAD_SIZE), jnp.float32), -6.0, 6.0)
    rows_of_keys = jnp.clip(jax.random.normal(jax.random.fold_in(key, 102), (TEACHER_BATCH, TEACHER_LENGTH, KEY_VALUE_HEADS, HEAD_SIZE), jnp.float32), -6.0, 6.0)
    return (rows_of_queries.reshape(TEACHER_BATCH, TEACHER_LENGTH, QUERY_HEADS * HEAD_SIZE), rows_of_keys.reshape(TEACHER_BATCH, TEACHER_LENGTH, KEY_VALUE_HEADS * HEAD_SIZE))


def draw_teacher_next_query(key, part):
    return teacher_pair(key)[0].astype(jnp.bfloat16)


def draw_teacher_next_key(key, part):
    return teacher_pair(key)[1].astype(jnp.bfloat16)


def draw_student_saved_query(key, part):
    values = jnp.clip(jax.random.normal(jax.random.fold_in(key, 107), (SBATCH, SLEN, QUERY_HEADS * HEAD_SIZE), jnp.float32), -6.0, 6.0)
    return values.astype(jnp.bfloat16)


def block_scale(key, shape, shards, low, largest):
    factor_of, own = 1.0, jax.random.fold_in(key, 6)
    for position, parts in shards:
        draws = jnp.exp(jax.random.uniform(jax.random.fold_in(own, position), (parts,), jnp.float32, low / len(shards), largest / len(shards)))
        factor_of = factor_of * jnp.repeat(draws, shape[position] // parts).reshape([-1 if axis == position else 1 for axis in range(len(shape))])
    return factor_of


def bell_draw(own_key, extent, scale, most, shards=(), held_as=jnp.bfloat16):
    entries = jax.random.normal(own_key, extent, jnp.float32) * scale
    if len(shards) > 0:
        entries = block_scale(own_key, extent, shards, -0.22, 0.18) * entries
    return jnp.clip(entries, min=-most, max=most).astype(held_as)


def setup_inputs(seed: int = 0) -> dict:
    key_of = jax.random.split(jax.random.key(seed), 11)
    student_saved_input = bell_draw(key_of[0], (SBATCH, SLEN, MODEL_WIDTH), 1.0, 6.0, ((0, 16), (1, 2)))
    student_saved_query = draw_student_saved_query(jax.random.fold_in(key_of[10], 71), 0)
    feature_cotangent = bell_draw(key_of[2], (SBATCH, SLEN, QUERY_HEADS * 2 * F), 1.0, 6.0, ((0, 16), (1, 2)))
    feature_weights = bell_draw(key_of[3], (HEAD_SIZE, QUERY_HEADS * F), HEAD_SIZE ** -0.5, 0.5)
    adapter_down_weight = bell_draw(key_of[4], (LOW_RANK, MODEL_WIDTH), MODEL_WIDTH ** -0.5, 0.09375)
    adapter_up_weight = bell_draw(key_of[5], (LOW_RANK, QUERY_HEADS * HEAD_SIZE), MODEL_WIDTH ** -0.5, 0.09375)
    teacher_next_query = draw_teacher_next_query(jax.random.fold_in(key_of[10], 71), 0)
    teacher_next_key = draw_teacher_next_key(jax.random.fold_in(key_of[10], 71), 0)
    teacher_next_value = bell_draw(key_of[8], (TEACHER_BATCH, TEACHER_LENGTH, KEY_VALUE_HEADS * HEAD_SIZE), 1.0, 6.0, ((0, 16), (1, 2)))
    positions = jax.vmap(lambda own: jax.random.permutation(own, TEACHER_LENGTH))(jax.random.split(key_of[9], TEACHER_BATCH)).reshape((TEACHER_BATCH, TEACHER_LENGTH)).astype(jnp.int32)
    return {"student_saved_input": student_saved_input, "student_saved_query": student_saved_query, "feature_cotangent": feature_cotangent, "feature_weights": feature_weights, "adapter_down_weight": adapter_down_weight, "adapter_up_weight": adapter_up_weight, "teacher_next_query": teacher_next_query, "teacher_next_key": teacher_next_key, "teacher_next_value": teacher_next_value, "positions": positions}


adapter_scale = 2.0
masked_score = -1e30


def teacher_one(operands):
    rows_of_queries, rows_of_keys, rows_of_values, pos_rows = operands
    group_width = QUERY_HEADS // KEY_VALUE_HEADS
    heads_of_queries = rows_of_queries.astype(jnp.float32).reshape(TEACHER_LENGTH, KEY_VALUE_HEADS, group_width, HEAD_SIZE)
    heads_of_keys = rows_of_keys.astype(jnp.float32).reshape(TEACHER_LENGTH, KEY_VALUE_HEADS, HEAD_SIZE)
    heads_of_values = rows_of_values.astype(jnp.float32).reshape(TEACHER_LENGTH, KEY_VALUE_HEADS, HEAD_SIZE)
    score = jnp.einsum("qcgd,kcd->cgqk", heads_of_queries, heads_of_keys, precision=lax.Precision.HIGHEST) * (HEAD_SIZE ** -0.5)
    allowed = (pos_rows[None, :] <= pos_rows[:, None])[None, None]
    score = jnp.where(allowed, score, masked_score)
    row_max = jnp.max(score, axis=-1)
    weight = jnp.where(allowed, jnp.exp(score - row_max[..., None]), 0.0)
    denom = jnp.sum(weight, axis=-1)
    weight_b = lax.optimization_barrier(weight.astype(jnp.bfloat16)).astype(jnp.float32)
    mixed = jnp.einsum("cgqk,kcd->qcgd", weight_b, heads_of_values, precision=lax.Precision.HIGHEST)
    output = mixed / jnp.transpose(denom, (2, 0, 1))[..., None]
    return output.astype(jnp.bfloat16).reshape(TEACHER_LENGTH, QUERY_HEADS * HEAD_SIZE)


def reference(student_saved_input, student_saved_query, feature_cotangent, feature_weights, adapter_down_weight, adapter_up_weight, teacher_next_query, teacher_next_key, teacher_next_value, positions):
    teacher_output = lax.map(teacher_one, (teacher_next_query, teacher_next_key, teacher_next_value, positions))
    row_count = SBATCH * SLEN
    heads_of_queries = student_saved_query.astype(jnp.float32).reshape(row_count, QUERY_HEADS, HEAD_SIZE)
    map_heads = feature_weights.astype(jnp.float32).reshape(HEAD_SIZE, QUERY_HEADS, F)
    logits = jnp.einsum("shd,dhf->shf", heads_of_queries, map_heads, precision=lax.Precision.HIGHEST)
    prob_plus = jax.nn.softmax(logits, axis=-1)
    prob_minus = jax.nn.softmax(-logits, axis=-1)
    cotangent = feature_cotangent.astype(jnp.float32).reshape(row_count, QUERY_HEADS, 2 * F)
    cot_plus = cotangent[..., :F]
    cot_minus = cotangent[..., F:]
    dlogit = prob_plus * (cot_plus - jnp.sum(prob_plus * cot_plus, axis=-1, keepdims=True)) - prob_minus * (cot_minus - jnp.sum(prob_minus * cot_minus, axis=-1, keepdims=True))
    dlogit_b = lax.optimization_barrier(dlogit.astype(jnp.bfloat16)).astype(jnp.float32)
    grad_feature = jnp.einsum("shd,shf->dhf", heads_of_queries, dlogit_b, precision=lax.Precision.HIGHEST).reshape(HEAD_SIZE, QUERY_HEADS * F)
    query_gradient = jnp.einsum("shf,dhf->shd", dlogit_b, map_heads, precision=lax.Precision.HIGHEST).reshape(row_count, QUERY_HEADS * HEAD_SIZE).astype(jnp.bfloat16)
    input_rows = student_saved_input.reshape(row_count, MODEL_WIDTH)
    down_activation = jnp.dot(input_rows, adapter_down_weight.T, preferred_element_type=jnp.float32).astype(jnp.bfloat16)
    up_gradient = adapter_scale * jnp.dot(down_activation.T, query_gradient, preferred_element_type=jnp.float32)
    lowrank_gradient = (adapter_scale * jnp.dot(query_gradient, adapter_up_weight.T, preferred_element_type=jnp.float32)).astype(jnp.bfloat16)
    grad_down = jnp.dot(lowrank_gradient.T, input_rows, preferred_element_type=jnp.float32)
    return (teacher_output, grad_feature, grad_down, up_gradient)
```

```python
import math

import jax
import jax.numpy as jnp
from jax import lax
from jax.experimental import pallas as pl
from jax.experimental.pallas import tpu as pltpu
from jax.sharding import PartitionSpec as P

HEAD = 128
F = 64
ADAPTER_SCALE = 2.0
MASKED = -1e30
F32 = jnp.float32
BF16 = jnp.bfloat16


def dot(a, b, ca, cb):
    return lax.dot_general(a, b, (((ca,), (cb,)), ((), ())), preferred_element_type=F32)


def student_kernel(parts, q_hbm, fw_hbm, cot_hbm, x_hbm, dw_hbm, uw_hbm, out_ref,
                   q_ref, fw_ref, cot_ref, x_ref, dw_ref, uw_ref, dq_ref, gf_ref, gd_ref, up_ref, sems):
    copies = [
        pltpu.make_async_copy(src, dst, sems.at[i])
        for i, (src, dst) in enumerate((
            (fw_hbm, fw_ref), (q_hbm, q_ref), (cot_hbm, cot_ref),
            (dw_hbm, dw_ref), (uw_hbm, uw_ref), (x_hbm, x_ref)))
    ]
    for c in copies:
        c.start()
    for c in copies[:3]:
        c.wait()
    rows = q_ref.shape[0]
    pairs = fw_ref.shape[1] // (2 * F)
    low_w = lax.broadcasted_iota(jnp.int32, (HEAD, 2 * F), 1) < F
    low = lax.broadcasted_iota(jnp.int32, (rows, 2 * F), 1) < F

    def halves(op, value, fill):
        a = op(jnp.where(low, value, fill), axis=-1, keepdims=True)
        b = op(jnp.where(low, fill, value), axis=-1, keepdims=True)
        return jnp.where(low, a, b)

    def doubled_gradient(q, w, cot):
        z = dot(q, w, 1, 0)
        e = jnp.exp(z - halves(jnp.max, z, -jnp.inf))
        prob = e / halves(jnp.sum, e, 0.0)
        g = prob * (cot - halves(jnp.sum, prob * cot, 0.0))
        return g - pltpu.roll(g, F, 1)

    for p in range(pairs):
        w_pair = fw_ref[:, p * 2 * F:(p + 1) * 2 * F].astype(F32)
        w_roll = pltpu.roll(w_pair, F, 1)
        w_first = jnp.where(low_w, w_pair, -w_roll).astype(BF16)
        w_second = jnp.where(low_w, w_roll, -w_pair).astype(BF16)
        at = 2 * p * HEAD
        q_pair = q_ref[:, at:at + 2 * HEAD]
        cot = cot_ref[:, at:at + 2 * HEAD].astype(F32)
        first = doubled_gradient(q_pair[:, :HEAD], w_first, cot[:, :HEAD])
        second = doubled_gradient(q_pair[:, HEAD:], w_second, cot[:, HEAD:])
        d_pair = jnp.where(low, first, -second).astype(BF16)
        both = dot(q_pair, d_pair, 0, 0)
        gf_ref[:, p * 2 * F:(p + 1) * 2 * F] = jnp.where(low_w, both[:HEAD], both[HEAD:])
        w_top = jnp.where(low_w, w_pair, 0.0).astype(BF16)
        w_bottom = jnp.where(low_w, 0.0, w_pair).astype(BF16)
        dq_ref[:, at:at + HEAD] = dot(d_pair, w_top, 1, 1).astype(BF16)
        dq_ref[:, at + HEAD:at + 2 * HEAD] = dot(d_pair, w_bottom, 1, 1).astype(BF16)

    for c in copies[3:]:
        c.wait()
    dq = dq_ref[...]
    x = x_ref[...]
    down = dot(x, dw_ref[...], 1, 1).astype(BF16)
    up_ref[...] = ADAPTER_SCALE * dot(down, dq, 0, 0)
    low_grad = (ADAPTER_SCALE * dot(dq, uw_ref[...], 1, 1)).astype(BF16)
    gd_ref[...] = dot(low_grad, x, 0, 0)

    width = out_ref.shape[2]
    gd_part = gd_ref.shape[1] // parts
    up_part = up_ref.shape[1] // parts
    gf_part = gf_ref.shape[0] // parts
    rank = gd_ref.shape[0]

    def padded(v):
        if v.shape[1] == width:
            return v
        return jnp.concatenate([v, jnp.zeros((v.shape[0], width - v.shape[1]), F32)], axis=1)

    for k in range(parts):
        small = jnp.concatenate([
            padded(gd_ref[:, k * gd_part:(k + 1) * gd_part]),
            padded(up_ref[:, k * up_part:(k + 1) * up_part])], axis=0)
        out_ref[k, :2 * rank, :] = small.astype(BF16)
        out_ref[k, 2 * rank:, :] = gf_ref[k * gf_part:(k + 1) * gf_part, :].astype(BF16)


def student(parts, x, q, cot, fw, dw, uw):
    rows = x.shape[0] * x.shape[1]
    x, q, cot = (v.reshape(rows, v.shape[-1]) for v in (x, q, cot))
    rank = dw.shape[0]
    width = max(fw.shape[1], x.shape[1] // parts)
    shape = (parts, 2 * rank + HEAD // parts, width)
    any_space = pl.BlockSpec(memory_space=pl.ANY)
    operands = (q, fw, cot, x, dw, uw)
    return pl.pallas_call(
        lambda *refs: student_kernel(parts, *refs),
        out_shape=jax.ShapeDtypeStruct(shape, BF16),
        in_specs=[any_space] * 6,
        out_specs=pl.BlockSpec(memory_space=pltpu.VMEM),
        scratch_shapes=[pltpu.VMEM(v.shape, BF16) for v in operands] + [
            pltpu.VMEM((rows, q.shape[1]), BF16),
            pltpu.VMEM(fw.shape, F32),
            pltpu.VMEM(dw.shape, F32),
            pltpu.VMEM(uw.shape, F32),
            pltpu.SemaphoreType.DMA((6,)),
        ],
        name="student",
    )(*operands)


def teacher_kernel(blocks, group, aliased, *refs):
    qpos_ref, kpos_ref, q_ref = refs[:3]
    k_refs = refs[3:3 + blocks]
    v_refs = refs[3 + blocks:3 + 2 * blocks]
    o_ref, bias_ref = refs[-2:]
    scale = HEAD ** -0.5 * math.log2(math.e)
    bias_ref[...] = jnp.where(kpos_ref[...] <= qpos_ref[...], 0.0, MASKED)
    keys = jnp.concatenate([k[0] for k in k_refs], axis=0)
    values = jnp.concatenate([v[0] for v in v_refs], axis=0)
    for g in range(group):
        q = q_ref[0, :, g * HEAD:(g + 1) * HEAD]
        s = dot(q, keys, 1, 1) + bias_ref[...]
        m = jnp.max(s, axis=-1, keepdims=True)
        w = jnp.exp2((s - m) * scale)
        denom = jnp.sum(w, axis=-1, keepdims=True)
        o = dot(w.astype(BF16), values, 1, 0)
        o_ref[0, :, g * HEAD:(g + 1) * HEAD] = (o * (1.0 / denom)).astype(BF16)


def teacher(q, keys, values, qpos, kpos, first, count, previous):
    blocks = len(keys)
    _, rows, key_width = keys[0].shape
    kv_heads = key_width // HEAD
    group = q.shape[2] // HEAD // kv_heads
    q_spec = pl.BlockSpec((1, q.shape[1], group * HEAD), lambda c: (0, 0, c + first))
    kv_spec = pl.BlockSpec((1, rows, HEAD), lambda c: (0, 0, c + first))
    whole = lambda v: pl.BlockSpec(v.shape, lambda c: (0, 0))
    operands = [qpos, kpos, q, *keys, *values]
    in_specs = [whole(qpos), whole(kpos), q_spec] + [kv_spec] * (2 * blocks)
    aliases = {}
    if previous is not None:
        aliases = {len(operands): 0}
        operands.append(previous)
        in_specs.append(pl.BlockSpec(memory_space=pl.ANY))
    return pl.pallas_call(
        lambda *refs: teacher_kernel(blocks, group, previous is not None, *refs),
        out_shape=jax.ShapeDtypeStruct(q.shape, BF16),
        grid=(count,),
        in_specs=in_specs,
        out_specs=q_spec,
        scratch_shapes=[pltpu.VMEM((q.shape[1], rows * blocks), F32)],
        input_output_aliases=aliases,
        name=f"teacher{first}",
    )(*operands)


def rotate(value, axis, size, shift):
    return lax.ppermute(value, axis, [(k, (k + shift) % size) for k in range(size)])


def exchange(value, axis, size, stride):
    return lax.ppermute(value, axis, [(k, k ^ stride) for k in range(size)])


def make_on_device(sizes):
    seq, dp, grp = sizes["seq"], sizes["dp"], sizes["grp"]

    def on_device(x, sq, cot, fw, dw, uw, tq, tk, tv, positions):
        pack = [(rotate(tk, "seq", seq, s), rotate(tv, "seq", seq, s), rotate(positions, "seq", seq, s))
                for s in range(1, seq)]
        keys = [tk] + [v[0] for v in pack]
        values = [tv] + [v[1] for v in pack]
        kpos = jnp.concatenate([positions] + [v[2] for v in pack], axis=1)
        qpos = positions.reshape(-1, 1)

        grads = student(dp, x, sq, cot, fw, dw, uw)
        mine = lax.axis_index("dp")
        kept = lax.dynamic_index_in_dim(grads, mine, 0, False)
        total = kept.astype(F32)
        for s in range(1, dp):
            piece = lax.dynamic_index_in_dim(grads, (mine + s) % dp, 0, False)
            total = total + rotate(piece, "dp", dp, s).astype(F32)

        kv_heads = tk.shape[2] // HEAD
        out = None
        for c in range(kv_heads):
            out = teacher(tq, keys, values, qpos, kpos, c, 1, out)

        for axis, size in (("seq", seq), ("grp", grp)):
            stride = 1
            while stride < size:
                total = total + exchange(total.astype(BF16), axis, size, stride).astype(F32)
                stride *= 2
        rank = dw.shape[0]
        grad_down = total[:rank, :x.shape[2] // dp]
        up = total[rank:2 * rank, :sq.shape[2] // dp]
        grad_feature = total[2 * rank:, :fw.shape[1]]
        return out, grad_feature, grad_down, up

    return on_device


def solution(mesh):
    tokens = P(("grp", "dp"), "seq", None)
    return jax.shard_map(
        make_on_device(dict(mesh.shape)),
        mesh=mesh,
        in_specs=(tokens, tokens, tokens, P(), P(), P(), tokens, tokens, tokens, P(("grp", "dp"), "seq")),
        out_specs=(tokens, P("dp", None), P(None, "dp"), P(None, "dp")),
        check_vma=False,
    )
```

```python
import math

import jax
import jax.numpy as jnp
from jax import lax
from jax.experimental import pallas as pl
from jax.experimental.pallas import tpu as pltpu
from jax.sharding import PartitionSpec as P

HEAD = 128
F = 64
ADAPTER_SCALE = 2.0
MASKED = -1e30
F32 = jnp.float32
BF16 = jnp.bfloat16


def dot(a, b, ca, cb):
    return lax.dot_general(a, b, (((ca,), (cb,)), ((), ())), preferred_element_type=F32)


def student_kernel(parts, q_hbm, fw_hbm, cot_hbm, x_hbm, dw_hbm, uw_hbm, pack_ref,
                   q_ref, fw_ref, cot_ref, x_ref, dw_ref, uw_ref, dq_ref, gd_ref, up_ref, sems):
    copies = [
        pltpu.make_async_copy(src, dst, sems.at[i])
        for i, (src, dst) in enumerate((
            (fw_hbm, fw_ref), (q_hbm, q_ref), (cot_hbm, cot_ref),
            (dw_hbm, dw_ref), (uw_hbm, uw_ref), (x_hbm, x_ref)))
    ]
    for c in copies:
        c.start()
    for c in copies[:3]:
        c.wait()
    pairs = fw_ref.shape[1] // (2 * F)
    rank = gd_ref.shape[0]
    gf_part = HEAD // parts
    low_w = lax.broadcasted_iota(jnp.int32, (HEAD, 2 * F), 1) < F
    eye = identity(2 * HEAD)

    def side(e, cot):
        inverse = 1.0 / jnp.sum(e, axis=0, keepdims=True)
        mean = jnp.sum(e * cot, axis=0, keepdims=True) * inverse
        return e * inverse * (cot - mean)

    for p in range(pairs):
        at = 2 * p * HEAD
        w_pair = fw_ref[:, p * 2 * F:(p + 1) * 2 * F].astype(F32)
        w_both = jnp.concatenate(
            [jnp.where(low_w, w_pair, 0.0), jnp.where(low_w, 0.0, w_pair)], axis=0).astype(BF16)
        q_pair = q_ref[:, at:at + 2 * HEAD]
        logit = dot(w_both, q_pair, 0, 1)
        cot = dot(eye, cot_ref[:, at:at + 2 * HEAD], 1, 1)
        grads = []
        for h in range(2):
            z = logit[h * F:(h + 1) * F]
            cot_plus = cot[2 * h * F:(2 * h + 1) * F]
            cot_minus = cot[(2 * h + 1) * F:(2 * h + 2) * F]
            plus = jnp.exp(z - jnp.max(z, axis=0, keepdims=True))
            minus = jnp.exp(jnp.min(z, axis=0, keepdims=True) - z)
            grads.append(side(plus, cot_plus) - side(minus, cot_minus))
        d_pair = jnp.concatenate(grads, axis=0).astype(BF16)
        dq_ref[:, at:at + 2 * HEAD] = dot(d_pair, w_both, 0, 1).astype(BF16)
        both = dot(d_pair, q_pair, 1, 0)
        map_grad = jnp.concatenate([both[:F, :HEAD], both[F:, HEAD:]], axis=0).astype(BF16)
        map_grad = dot(eye[:HEAD, :HEAD], map_grad, 1, 1)
        for k in range(parts):
            pack_ref[k, 2 * rank:, p * 2 * F:(p + 1) * 2 * F] = (
                map_grad[k * gf_part:(k + 1) * gf_part].astype(BF16))

    for c in copies[3:]:
        c.wait()
    dq = dq_ref[...]
    x = x_ref[...]
    down = dot(x, dw_ref[...], 1, 1).astype(BF16)
    up_ref[...] = ADAPTER_SCALE * dot(down, dq, 0, 0)
    low_grad = (ADAPTER_SCALE * dot(dq, uw_ref[...], 1, 1)).astype(BF16)
    gd_ref[...] = dot(low_grad, x, 0, 0)

    width = pack_ref.shape[2]
    gd_part = gd_ref.shape[1] // parts
    up_part = up_ref.shape[1] // parts

    def padded(v):
        if v.shape[1] == width:
            return v
        return jnp.concatenate([v, jnp.zeros((v.shape[0], width - v.shape[1]), F32)], axis=1)

    for k in range(parts):
        small = jnp.concatenate([
            padded(gd_ref[:, k * gd_part:(k + 1) * gd_part]),
            padded(up_ref[:, k * up_part:(k + 1) * up_part])], axis=0)
        pack_ref[k, :2 * rank, :] = small.astype(BF16)


def identity(n):
    return (lax.broadcasted_iota(jnp.int32, (n, n), 0)
            == lax.broadcasted_iota(jnp.int32, (n, n), 1)).astype(F32).astype(BF16)


def student(parts, x, q, cot, fw, dw, uw):
    rows = x.shape[0] * x.shape[1]
    x, q, cot = (v.reshape(rows, v.shape[-1]) for v in (x, q, cot))
    rank = dw.shape[0]
    width = max(fw.shape[1], x.shape[1] // parts)
    shape = (parts, 2 * rank + HEAD // parts, width)
    any_space = pl.BlockSpec(memory_space=pl.ANY)
    operands = (q, fw, cot, x, dw, uw)
    return pl.pallas_call(
        lambda *refs: student_kernel(parts, *refs),
        out_shape=jax.ShapeDtypeStruct(shape, BF16),
        in_specs=[any_space] * 6,
        out_specs=pl.BlockSpec(memory_space=pltpu.VMEM),
        scratch_shapes=[pltpu.VMEM(v.shape, BF16) for v in operands] + [
            pltpu.VMEM((rows, q.shape[1]), BF16),
            pltpu.VMEM(dw.shape, F32),
            pltpu.VMEM(uw.shape, F32),
            pltpu.SemaphoreType.DMA((6,)),
        ],
        name="student",
    )(*operands)


def teacher_kernel(blocks, group, *refs):
    qpos_ref, kpos_ref, q_ref = refs[:3]
    k_refs = refs[3:3 + blocks]
    v_refs = refs[3 + blocks:3 + 2 * blocks]
    o_ref, bias_ref = refs[-2:]
    scale = HEAD ** -0.5 * math.log2(math.e)
    bias_ref[...] = jnp.where(kpos_ref[...] <= qpos_ref[...], 0.0, MASKED)
    keys = jnp.concatenate([k[0] for k in k_refs], axis=0)
    values = jnp.concatenate([v[0] for v in v_refs], axis=0)
    for g in range(group):
        q = q_ref[0, :, g * HEAD:(g + 1) * HEAD]
        s = dot(q, keys, 1, 1) + bias_ref[...]
        m = jnp.max(s, axis=-1, keepdims=True)
        w = jnp.exp2((s - m) * scale)
        denom = jnp.sum(w, axis=-1, keepdims=True)
        o = dot(w.astype(BF16), values, 1, 0)
        o_ref[0, :, g * HEAD:(g + 1) * HEAD] = (o * (1.0 / denom)).astype(BF16)


def teacher(q, keys, values, qpos, kpos, first, count, previous):
    blocks = len(keys)
    _, rows, key_width = keys[0].shape
    kv_heads = key_width // HEAD
    group = q.shape[2] // HEAD // kv_heads
    q_spec = pl.BlockSpec((1, q.shape[1], group * HEAD), lambda c: (0, 0, c + first))
    kv_spec = pl.BlockSpec((1, rows, HEAD), lambda c: (0, 0, c + first))
    whole = lambda v: pl.BlockSpec(v.shape, lambda c: (0, 0))
    operands = [qpos, kpos, q, *keys, *values]
    in_specs = [whole(qpos), whole(kpos), q_spec] + [kv_spec] * (2 * blocks)
    aliases = {}
    if previous is not None:
        aliases = {len(operands): 0}
        operands.append(previous)
        in_specs.append(pl.BlockSpec(memory_space=pl.ANY))
    return pl.pallas_call(
        lambda *refs: teacher_kernel(blocks, group, *refs),
        out_shape=jax.ShapeDtypeStruct(q.shape, BF16),
        grid=(count,),
        in_specs=in_specs,
        out_specs=q_spec,
        scratch_shapes=[pltpu.VMEM((q.shape[1], rows * blocks), F32)],
        input_output_aliases=aliases,
    )(*operands)


def rotate(value, axis, size, shift):
    return lax.ppermute(value, axis, [(k, (k + shift) % size) for k in range(size)])


def exchange(value, axis, size, stride):
    return lax.ppermute(value, axis, [(k, k ^ stride) for k in range(size)])


def make_on_device(sizes):
    seq, dp, grp = sizes["seq"], sizes["dp"], sizes["grp"]

    def compute(x, sq, cot, fw, dw, uw, tq, tk, tv, positions):
        pack = []
        for s in range(1, seq):
            moved = []
            for v in (tk, tv, positions):
                moved.append(rotate(v, "seq", seq, s))
            pack.append(moved)
        keys = [tk] + [v[0] for v in pack]
        values = [tv] + [v[1] for v in pack]
        kpos = jnp.concatenate([positions] + [v[2] for v in pack], axis=1)
        qpos = positions.reshape(-1, 1)

        grads = student(dp, x, sq, cot, fw, dw, uw)
        mine = lax.axis_index("dp")
        total = lax.dynamic_index_in_dim(grads, mine, 0, False).astype(F32)
        for s in range(1, dp):
            piece = lax.dynamic_index_in_dim(grads, (mine + s) % dp, 0, False)
            piece = rotate(piece, "dp", dp, s)
            total = total + piece.astype(F32)

        kv_heads = tk.shape[2] // HEAD
        out = None
        for c in range(kv_heads):
            out = teacher(tq, keys, values, qpos, kpos, c, 1, out)

        for axis, size in (("seq", seq), ("grp", grp)):
            stride = 1
            while stride < size:
                moved = exchange(total.astype(BF16), axis, size, stride)
                total = total + moved.astype(F32)
                stride *= 2
        rank = dw.shape[0]
        grad_down = total[:rank, :x.shape[2] // dp]
        up = total[rank:2 * rank, :sq.shape[2] // dp]
        grad_feature = total[2 * rank:, :fw.shape[1]]
        return out, grad_feature, grad_down, up

    return compute


def solution(mesh):
    tokens = P(("grp", "dp"), "seq", None)
    sizes = dict(mesh.shape)
    return jax.shard_map(
        make_on_device(sizes),
        mesh=mesh,
        in_specs=(tokens, tokens, tokens, P(), P(), P(), tokens, tokens, tokens, P(("grp", "dp"), "seq")),
        out_specs=(tokens, P("dp", None), P(None, "dp"), P(None, "dp")),
        check_vma=False,
    )
```
